512 devices in a mesh: clus: 32 (over y, x, core), dir: 16 (over z).
Axes of the slice: x: 4, y: 4, z: 16, core: 2. Of those that a mesh axis runs over, the one named last changes fastest.
Arguments:
- sources: bfloat16 [96, 524288], P(None, ('clus', 'dir')), may hold values from -6 to 6
- live_counts: int32 [32, 16], P('clus'), may hold values from 1 to 16, 128 in all within a row
- aggregate: bfloat16 [512, 96], replicated, may hold values from -0.625 to 0.625
- translators: bfloat16 [316, 512], P(None, 'dir'), may hold values from -0.21875 to 0.21875
- boundary_lists: int32 [32, 2, 32], P('clus'), may hold values from 0 to 255
- far_sources: int32 [8192, 128], P('clus'), may hold values from 0 to 319
- far_translators: int32 [8192, 128], P('clus'), may hold values from 0 to 315
- near_blocks: bfloat16 [8192, 96, 576], P(('clus', 'dir')), may hold values from -0.25 to 0.25
- near_columns: int32 [8192, 6], P(('clus', 'dir')), may hold values from 0 to 15
Outputs:
- field: bfloat16 [96, 524288], P(None, ('clus', 'dir'))
The draws below stay inside these ranges and needn't reach their ends.
Inputs may be any that keep to these rules, and one draw needn't show every extreme that they name: `live_counts`: A cluster's counts add to 128; in every cluster some device holds all 16 of its slots. `far_sources`: values below 256 name the cluster's own slots, the next 32 the boxes received from the previous cluster, the last 32 those from the next cluster.
All inputs are finite; a program needn't handle non-finite values.
Results may differ from the reference program's by a relative error of at most 0.0075.
Values may be sent and summed in bfloat16 or wider, within the bound.
No kernel may reach another device: no remote copies, remote signals or barrier semaphores. Data moves between devices by JAX's collectives and lax.ppermute only.
A program may use at most 64 MiB of HBM per device.

```python
import math
import jax
import jax.numpy as jnp
import numpy as np
from jax import lax

U = 96
K = 512
R = 64
NTR = 316
NI = 128
NN = 6
NBND = 32
BCAP = 16
BOX_CL = 128
S_CL = 256
S_EXT = 320
SLOTS = 8192
N_CLUS = 32
N_DIR = 16


def place_ends(entries, key, low, high):
    longest = entries.shape.index(max(entries.shape))
    spots = []
    for shift in (0, 1):
        where = [jax.random.randint(jax.random.fold_in(key, axis), (), 0, length) for axis, length in enumerate(entries.shape)]
        where[longest] = (where[longest] + shift) % entries.shape[longest]
        spots.append(tuple(where))
    return entries.at[spots[0]].set(low).at[spots[1]].set(high)


def level_of(rng, extent, pieces, low, top_value):
    def one(dim, blocks):
        draws = jax.random.uniform(jax.random.fold_in(jax.random.fold_in(rng, 6), dim), (blocks,), jnp.float32, low / len(pieces), top_value / len(pieces))
        return jnp.repeat(jnp.exp(draws), extent[dim] // blocks).reshape((-1,) + (1,) * (len(extent) - dim - 1))

    gain = one(*pieces[0])
    for cut in pieces[1:]:
        gain = gain * one(*cut)
    return gain


def profile(count, total, most, lean):
    portions = [(1 << 20) // math.isqrt(grade ** lean) + 1 for grade in range(2, count + 1)]
    surplus, given = total - most - (count - 1), [1] * (count - 1)
    while surplus > 0:
        free = [i for i in range(count - 1) if given[i] < most]
        mass, remaining = sum([portions[i] for i in free]), surplus
        for i in free:
            addition = min(most - given[i], max(1, remaining * portions[i] // mass), surplus)
            given[i] = given[i] + addition
            surplus = surplus - addition
    return np.array([most] + given)


def ragged_sizes(rng, amount, total, most, skew):
    if amount == 2:
        one = jax.random.randint(rng, (), max(1, total - most), min(most, total - 1) + 1)
        return jnp.stack([one, total - one])
    tallies = jnp.asarray(profile(amount, total, most, skew), jnp.int32)
    twos = (amount - 1) // 2
    donor, sink = tallies[1:1 + 2 * twos:2], tallies[2:2 + 2 * twos:2]
    margin = jnp.minimum(donor - 1, most - sink)
    shifted = jax.random.randint(jax.random.fold_in(rng, 1), (twos,), 0, 1 << 20) % (margin + 1)
    tallies = tallies.at[1:1 + 2 * twos:2].set(donor - shifted).at[2:2 + 2 * twos:2].set(sink + shifted)
    return tallies[jax.random.permutation(jax.random.fold_in(rng, 2), amount)]


def noise(rng, shape, width, limit, split=(), held_as=jnp.bfloat16):
    array = width * jax.random.normal(rng, shape, jnp.float32)
    if split:
        array = array * level_of(rng, shape, split, -0.22, 0.18)
    return jnp.clip(array, -limit, limit).astype(held_as)


def setup_inputs(seed: int = 0) -> dict:
    keys = jax.random.split(jax.random.key(seed), 10)
    return {
        "sources": noise(keys[0], (U, SLOTS * R), 1.0, 6.0, ((1, 512),)),
        "live_counts": jax.vmap(lambda own: ragged_sizes(own, N_DIR, BOX_CL, BCAP, 2))(jax.random.split(keys[1], N_CLUS)).reshape((N_CLUS, N_DIR)).astype(jnp.int32),
        "aggregate": noise(keys[2], (K, U), U ** -0.5, 0.625),
        "translators": noise(keys[3], (NTR, K), (NI * K // U) ** -0.5, 0.21875, ((1, 16),)),
        "boundary_lists": place_ends(jax.random.randint(keys[4], (N_CLUS, 2, NBND), 0, S_CL), jax.random.fold_in(keys[4], 1), 0, S_CL - 1).astype(jnp.int32),
        "far_sources": place_ends(jax.random.randint(keys[5], (SLOTS, NI), 0, S_EXT), jax.random.fold_in(keys[5], 1), 0, S_EXT - 1).astype(jnp.int32),
        "far_translators": place_ends(jax.random.randint(keys[6], (SLOTS, NI), 0, NTR), jax.random.fold_in(keys[6], 1), 0, NTR - 1).astype(jnp.int32),
        "near_blocks": noise(keys[7], (SLOTS, U, NN * U), (NN * U) ** -0.5, 0.25, ((0, 512),)),
        "near_columns": place_ends(jax.random.randint(keys[8], (SLOTS, NN), 0, BCAP), jax.random.fold_in(keys[8], 1), 0, BCAP - 1).astype(jnp.int32),
    }


def reference(sources, live_counts, aggregate, translators, boundary_lists, far_sources, far_translators, near_blocks, near_columns):
    live_mask = (jnp.arange(BCAP, dtype=jnp.int32)[None, None, :] < live_counts[:, :, None]).reshape(SLOTS)
    masked = sources.reshape(U, SLOTS, R) * live_mask.astype(jnp.bfloat16)[None, :, None]
    pattern = jnp.dot(aggregate, masked.reshape(U, SLOTS * R), preferred_element_type=jnp.float32).astype(jnp.bfloat16)
    pattern = pattern.reshape(K, N_CLUS, S_CL, R)
    empty_block = jnp.zeros((K, 1, S_CL, R), jnp.bfloat16)
    padded = jnp.concatenate([empty_block, pattern, empty_block], axis=1)
    empty_list = jnp.zeros((1, 2, NBND), jnp.int32)
    padded_lists = jnp.concatenate([empty_list, boundary_lists, empty_list], axis=0)
    kind_table = translators.astype(jnp.float32)
    target_rows = jnp.broadcast_to(jnp.arange(S_CL, dtype=jnp.int32)[:, None], (S_CL, NI))
    slot_base = (jnp.arange(S_CL, dtype=jnp.int32) // BCAP) * BCAP

    def cluster_field(cluster):
        own_block = lax.dynamic_index_in_dim(padded, cluster + 1, 1, keepdims=False)
        before = lax.dynamic_index_in_dim(padded, cluster, 1, keepdims=False)
        following = lax.dynamic_index_in_dim(padded, cluster + 2, 1, keepdims=False)
        before_list = lax.dynamic_index_in_dim(padded_lists, cluster, 0, keepdims=False)[0]
        following_list = lax.dynamic_index_in_dim(padded_lists, cluster + 2, 0, keepdims=False)[1]
        extended = jnp.concatenate([own_block, before[:, before_list, :], following[:, following_list, :]], axis=1).astype(jnp.float32)
        first_row = cluster * S_CL
        sources_here = lax.dynamic_slice_in_dim(far_sources, first_row, S_CL, 0)
        kinds_here = lax.dynamic_slice_in_dim(far_translators, first_row, S_CL, 0)
        weights = jnp.zeros((S_CL, S_EXT, K), jnp.float32).at[target_rows, sources_here].add(kind_table[kinds_here])
        incoming = jnp.einsum("tsk,ksr->ktr", weights, extended, precision=lax.Precision.HIGHEST).astype(jnp.bfloat16)
        far_part = jnp.dot(aggregate.T, incoming.reshape(K, S_CL * R), preferred_element_type=jnp.float32)
        local_units = lax.dynamic_slice_in_dim(masked, first_row, S_CL, 1)
        neighbour_slots = lax.dynamic_slice_in_dim(near_columns, first_row, S_CL, 0) + slot_base[:, None]
        stacked = local_units[:, neighbour_slots, :].astype(jnp.float32)
        blocks = lax.dynamic_slice_in_dim(near_blocks, first_row, S_CL, 0).astype(jnp.float32).reshape(S_CL, U, NN, U)
        near_part = jnp.einsum("sujv,vsjr->usr", blocks, stacked, precision=lax.Precision.HIGHEST)
        return far_part + near_part.reshape(U, S_CL * R)

    fields = lax.map(cluster_field, jnp.arange(N_CLUS, dtype=jnp.int32))
    summed = fields.transpose(1, 0, 2).reshape(U, SLOTS, R) * live_mask.astype(jnp.float32)[None, :, None]
    return summed.reshape(U, SLOTS * R).astype(jnp.bfloat16)
```

```python
import jax
import jax.numpy as jnp
from jax import lax
from jax.experimental import pallas as pl
from jax.experimental.pallas import tpu as pltpu
from jax.sharding import PartitionSpec as P

U = 96
K = 512
R = 64
NTR = 316
NI = 128
NN = 6
NBND = 32
BCAP = 16
S_CL = 256
S_EXT = 320
N_DIR = 16
RD = R // N_DIR
KC = K // 128
NTR_PAD = 320
F32 = jnp.float32
BF16 = jnp.bfloat16


def shifted(value, axis, steps):
    count = lax.axis_size(axis)
    leading, last = (max(0, -steps), min(count, count - steps))
    return lax.ppermute(value, axis, [(source, source + steps) for source in range(leading, last)])


def deal_kernel(src_ref, out_ref, rows):
    for pair in range(BCAP // 2):
        turned = src_ref[:, pair * 128 : (pair + 1) * 128].astype(F32).T
        for half in range(2):
            rows[pl.ds(2 * pair + half, R, stride=BCAP), :] = turned[half * R : (half + 1) * R]
    out_ref[...] = rows[...].reshape(N_DIR, RD, BCAP, U).astype(BF16)


def boundary_kernel(recv_ref, list_ref, live_ref, up_ref, down_ref):
    slots = lax.broadcasted_iota(jnp.int32, (2 * NBND, S_CL), 1)
    pick = ((slots == list_ref[...]) & (live_ref[...] > 0)).astype(F32).astype(BF16)
    for r in range(RD):
        units = recv_ref[:, r].reshape(S_CL, U)
        chosen = jnp.dot(pick, units, preferred_element_type=F32).astype(BF16)
        up_ref[r] = chosen[:NBND]
        down_ref[r] = chosen[NBND:]


def far_kernel(
    pairs, counts, recv_ref, live_ref, before_ref, after_ref, kinds_ref, agg_ref, out_ref, ext, table, incoming
):
    agg = agg_ref[...]
    for r in range(RD):
        own = jnp.dot(recv_ref[:, r].reshape(S_CL, U), agg, preferred_element_type=F32)
        own = jnp.where(live_ref[...] > 0, own, 0.0)
        prev = jnp.dot(before_ref[r], agg, preferred_element_type=F32)
        foll = jnp.dot(after_ref[r], agg, preferred_element_type=F32)
        for c in range(KC):
            lanes = slice(c * 128, (c + 1) * 128)
            at = r * KC + c
            ext[pl.ds(at, S_CL, stride=16), :] = own[:, lanes]
            ext[pl.ds(S_CL * 16 + at, NBND, stride=16), :] = prev[:, lanes]
            ext[pl.ds((S_CL + NBND) * 16 + at, NBND, stride=16), :] = foll[:, lanes]
    eye = lax.broadcasted_iota(jnp.int32, (NTR_PAD, NTR), 0) == lax.broadcasted_iota(
        jnp.int32, (NTR_PAD, NTR), 1
    )
    kinds = lax.dot_general(
        eye.astype(F32).astype(BF16),
        kinds_ref[...],
        (((1,), (1,)), ((), ())),
        preferred_element_type=F32,
    )
    for c in range(KC):
        part = kinds[:, c * 128 : (c + 1) * 128]
        table[pl.ds(c, NTR_PAD, stride=8), :] = part
        table[pl.ds(c + KC, NTR_PAD, stride=8), :] = part
    incoming[...] = jnp.zeros_like(incoming)

    def device(d, carry):
        def target(j, inner):
            t = d * BCAP + j
            sums = [[jnp.zeros((8, 128), F32) for _ in range(2)] for _ in range(2)]
            for i in range(NI):
                word = pairs[t, i]
                n8 = pl.multiple_of(word & 0xFFFF, 8)
                s16 = pl.multiple_of(lax.shift_right_logical(word, 16), 16)
                weight = table[pl.ds(n8, 8), :]
                for h in range(2):
                    sums[i % 2][h] = sums[i % 2][h] + weight * ext[pl.ds(s16 + 8 * h, 8), :]
            for h in range(2):
                incoming[pl.ds(pl.multiple_of(t * 16 + 8 * h, 8), 8), :] = sums[0][h] + sums[1][h]
            return inner

        return lax.fori_loop(0, counts[d], target, carry)

    lax.fori_loop(0, N_DIR, device, 0)
    for r in range(RD):
        far = jnp.zeros((S_CL, U), F32)
        for c in range(KC):
            part = incoming[pl.ds(r * KC + c, S_CL, stride=16), :].astype(BF16)
            far = far + lax.dot_general(
                part,
                agg[:, c * 128 : (c + 1) * 128],
                (((1,), (1,)), ((), ())),
                preferred_element_type=F32,
            )
        out_ref[:, r] = far.reshape(N_DIR, BCAP, U).astype(BF16)


def near_kernel(columns, count, src_ref, blocks_ref, out_ref, units, stack):
    for pair in range(BCAP // 2):
        both = src_ref[:, pair * 128 : (pair + 1) * 128].astype(F32)
        for half in range(2):
            slot = 2 * pair + half
            own = both[:, half * R : (half + 1) * R]
            units[slot] = jnp.where(count[0] > slot, own, 0.0).astype(BF16)
    for pair in range(BCAP // 2):
        halves = []
        for half in range(2):
            slot = 2 * pair + half
            for j in range(NN):
                stack[j * U : (j + 1) * U, :] = units[columns[slot, j]]
            halves.append(jnp.dot(blocks_ref[slot], stack[...], preferred_element_type=F32))
        out_ref[:, pair * 128 : (pair + 1) * 128] = jnp.concatenate(halves, axis=1)


def finish_kernel(count, back_ref, near_ref, out_ref, rows):
    rows[...] = back_ref[...].astype(F32).reshape(R * BCAP, U)
    for pair in range(BCAP // 2):
        halves = [rows[pl.ds(2 * pair + half, R, stride=BCAP), :] for half in range(2)]
        far = jnp.concatenate(halves, axis=0).T
        cols = slice(pair * 128, (pair + 1) * 128)
        slot = 2 * pair + lax.broadcasted_iota(jnp.int32, (U, 128), 1) // R
        out_ref[:, cols] = jnp.where(slot < count[0], far + near_ref[:, cols], 0.0).astype(BF16)


VM = pl.BlockSpec(memory_space=pltpu.VMEM)
SM = pl.BlockSpec(memory_space=pltpu.SMEM)


def per_device(
    sources,
    live_counts,
    aggregate,
    translators,
    boundary_lists,
    far_sources,
    far_translators,
    near_blocks,
    near_columns,
):
    dir_index = lax.axis_index("dir")
    counts = live_counts[0]
    own_count = lax.dynamic_slice(counts, (dir_index,), (1,))
    slot_ids = jnp.arange(S_CL, dtype=jnp.int32)
    live = (slot_ids % BCAP < jnp.repeat(counts, BCAP)).astype(jnp.int32)

    send = pl.pallas_call(
        deal_kernel,
        out_shape=jax.ShapeDtypeStruct((N_DIR, RD, BCAP, U), BF16),
        in_specs=[VM],
        out_specs=VM,
        scratch_shapes=[pltpu.VMEM((R * BCAP, U), F32)],
        name="deal",
    )(sources)
    recv = lax.all_to_all(send, "dir", split_axis=0, concat_axis=0, tiled=True)
    kinds = lax.all_to_all(
        jnp.broadcast_to(translators.T[None], (N_DIR, K // N_DIR, NTR)),
        "dir",
        split_axis=0,
        concat_axis=0,
        tiled=True,
    ).reshape(K, NTR)

    up, down = pl.pallas_call(
        boundary_kernel,
        out_shape=[jax.ShapeDtypeStruct((RD, NBND, U), BF16)] * 2,
        in_specs=[VM, VM, VM],
        out_specs=[VM, VM],
        name="boundary",
    )(recv, boundary_lists.reshape(2 * NBND, 1), live.reshape(1, S_CL))
    before = shifted(up, "clus", 1)
    after = shifted(down, "clus", -1)

    near = pl.pallas_call(
        near_kernel,
        out_shape=jax.ShapeDtypeStruct((U, BCAP * R), F32),
        in_specs=[SM, SM, VM, VM],
        out_specs=VM,
        scratch_shapes=[pltpu.VMEM((BCAP, U, R), BF16), pltpu.VMEM((NN * U, R), BF16)],
        name="near",
    )(near_columns, own_count, sources, near_blocks)

    pairs = far_sources * (16 << 16) + far_translators * 8
    far = pl.pallas_call(
        far_kernel,
        out_shape=jax.ShapeDtypeStruct((N_DIR, RD, BCAP, U), BF16),
        in_specs=[SM, SM, VM, VM, VM, VM, VM, VM],
        out_specs=VM,
        scratch_shapes=[
            pltpu.VMEM((S_EXT * 16, 128), F32),
            pltpu.VMEM((NTR_PAD * 8, 128), F32),
            pltpu.VMEM((S_CL * 16, 128), F32),
        ],
        name="far",
    )(pairs, counts, recv, live.reshape(S_CL, 1), before, after, kinds, aggregate.T)
    back = lax.all_to_all(far, "dir", split_axis=0, concat_axis=0, tiled=True)

    return pl.pallas_call(
        finish_kernel,
        out_shape=jax.ShapeDtypeStruct((U, BCAP * R), BF16),
        in_specs=[SM, VM, VM],
        out_specs=VM,
        scratch_shapes=[pltpu.VMEM((R * BCAP, U), F32)],
        name="finish",
    )(own_count, back, near)


def solution(mesh):
    in_specs = (
        P(None, ("clus", "dir")),
        P("clus", None),
        P(),
        P(None, "dir"),
        P("clus", None, None),
        P("clus", None),
        P("clus", None),
        P(("clus", "dir"), None, None),
        P(("clus", "dir"), None),
    )
    out_specs = P(None, ("clus", "dir"))
    return jax.shard_map(
        per_device, mesh=mesh, in_specs=in_specs, out_specs=out_specs, check_vma=False
    )
```

```python
import jax
import jax.numpy as jnp
from jax import lax
from jax.experimental import pallas as pl
from jax.experimental.pallas import tpu as pltpu
from jax.sharding import PartitionSpec as P

U = 96
K = 512
R = 64
NTR = 316
NI = 128
NN = 6
NBND = 32
BCAP = 16
S_CL = 256
S_EXT = 320
N_DIR = 16
KD = K // N_DIR
RD = R // N_DIR
KC = K // 128
NTR_PAD = 320
LAST = (S_CL - 1) * NI + 1
F32 = jnp.float32
BF16 = jnp.bfloat16


def shifted(value, axis, steps):
    count = lax.axis_size(axis)
    leading, last = (max(0, -steps), min(count, count - steps))
    return lax.ppermute(value, axis, [(source, source + steps) for source in range(leading, last)])


def deal_kernel(src_ref, kinds_ref, out_ref, rows, wide):
    for pair in range(BCAP // 2):
        both = src_ref[:, pair * 128 : (pair + 1) * 128].astype(F32)
        both = jnp.concatenate([both, jnp.zeros((128 - U, 128), F32)], axis=0).T
        for half in range(2):
            rows[pl.ds(2 * pair + half, R, stride=BCAP), :] = both[half * R : (half + 1) * R]
    wide[...] = jnp.zeros_like(wide)
    wide[:, :NTR] = kinds_ref[...].astype(F32)
    last = wide[:, 256:384]
    spare = jnp.concatenate([pltpu.roll(last, U, 1), pltpu.roll(last, U - KD, 1)], axis=0)
    in_spare = lax.broadcasted_iota(jnp.int32, (RD * BCAP, 128), 1) >= U
    tail = jnp.concatenate([wide[:, :128], wide[:, 128:256]], axis=0).astype(BF16)
    for d in range(N_DIR):
        block = rows[d * RD * BCAP : (d + 1) * RD * BCAP, :]
        out_ref[d, : RD * BCAP] = jnp.where(in_spare, spare, block).astype(BF16)
        out_ref[d, RD * BCAP :] = tail


def units_of(recv_ref, r):
    return recv_ref[:, r * BCAP : (r + 1) * BCAP].reshape(S_CL, 128)


def boundary_kernel(recv_ref, list_ref, live_ref, up_ref, down_ref):
    slots = lax.broadcasted_iota(jnp.int32, (2 * NBND, S_CL), 1)
    pick = ((slots == list_ref[...]) & (live_ref[...] > 0)).astype(F32).astype(BF16)
    for r in range(RD):
        chosen = jnp.dot(pick, units_of(recv_ref, r), preferred_element_type=F32).astype(BF16)
        up_ref[r] = chosen[:NBND]
        down_ref[r] = chosen[NBND:]


def far_kernel(
    kind_rows,
    source_rows,
    counts,
    recv_ref,
    live_ref,
    before_ref,
    after_ref,
    agg_ref,
    out_ref,
    ext,
    table,
    incoming,
):
    agg = agg_ref[...]
    for r in range(RD):
        own = jnp.dot(units_of(recv_ref, r), agg, preferred_element_type=F32)
        own = jnp.where(live_ref[...] > 0, own, 0.0)
        prev = jnp.dot(before_ref[r], agg, preferred_element_type=F32)
        foll = jnp.dot(after_ref[r], agg, preferred_element_type=F32)
        for c in range(KC):
            lanes = slice(c * 128, (c + 1) * 128)
            at = r * KC + c
            ext[pl.ds(at, S_CL, stride=16), :] = own[:, lanes]
            ext[pl.ds(S_CL * 16 + at, NBND, stride=16), :] = prev[:, lanes]
            ext[pl.ds((S_CL + NBND) * 16 + at, NBND, stride=16), :] = foll[:, lanes]
    for first, count, lane, row in ((0, 128, 0, 64), (128, 128, 0, 96), (256, 32, U, 0), (288, 32, U, 32)):
        pick = lax.broadcasted_iota(jnp.int32, (count, 128), 0) + lane == lax.broadcasted_iota(
            jnp.int32, (count, 128), 1
        )
        kinds = lax.dot_general(
            pick.astype(F32).astype(BF16),
            recv_ref[:, row : row + KD].reshape(K, 128),
            (((1,), (1,)), ((), ())),
            preferred_element_type=F32,
        )
        for c in range(KC):
            part = kinds[:, c * 128 : (c + 1) * 128]
            table[pl.ds(first * 8 + c, count, stride=8), :] = part
            table[pl.ds(first * 8 + c + KC, count, stride=8), :] = part
    incoming[...] = jnp.zeros_like(incoming)

    def device(d, carry):
        def target(j, inner):
            t = d * BCAP + j
            first = t * NI
            sums = [[jnp.zeros((8, 128), F32) for _ in range(2)] for _ in range(2)]
            for i in range(NI):
                n8 = pl.multiple_of(kind_rows.at[pl.ds(i, LAST)][first], 8)
                s16 = pl.multiple_of(source_rows.at[pl.ds(i, LAST)][first], 16)
                weight = table[pl.ds(n8, 8), :]
                for h in range(2):
                    sums[i % 2][h] = sums[i % 2][h] + weight * ext[pl.ds(s16 + 8 * h, 8), :]
            for h in range(2):
                incoming[pl.ds(pl.multiple_of(t * 16 + 8 * h, 8), 8), :] = sums[0][h] + sums[1][h]
            return inner

        return lax.fori_loop(0, counts[d], target, carry)

    lax.fori_loop(0, N_DIR, device, 0)
    for r in range(RD):
        far = jnp.zeros((S_CL, U), F32)
        for c in range(KC):
            part = incoming[pl.ds(r * KC + c, S_CL, stride=16), :].astype(BF16)
            far = far + lax.dot_general(
                part,
                agg[:U, c * 128 : (c + 1) * 128],
                (((1,), (1,)), ((), ())),
                preferred_element_type=F32,
            )
        out_ref[:, r] = far.reshape(N_DIR, BCAP, U).astype(BF16)


def near_kernel(columns, count, src_ref, blocks_ref, out_ref, units, stack):
    for pair in range(BCAP // 2):
        both = src_ref[:, pair * 128 : (pair + 1) * 128].astype(F32)
        for half in range(2):
            slot = 2 * pair + half
            own = both[:, half * R : (half + 1) * R]
            units[slot] = jnp.where(count[0] > slot, own, 0.0).astype(BF16)
    for pair in range(BCAP // 2):
        halves = []
        for half in range(2):
            slot = 2 * pair + half
            for j in range(NN):
                stack[j * U : (j + 1) * U, :] = units[columns[slot, j]]
            halves.append(jnp.dot(blocks_ref[slot], stack[...], preferred_element_type=F32))
        out_ref[:, pair * 128 : (pair + 1) * 128] = jnp.concatenate(halves, axis=1)


def finish_kernel(count, back_ref, near_ref, out_ref, rows):
    rows[...] = back_ref[...].astype(F32).reshape(R * BCAP, U)
    for pair in range(BCAP // 2):
        halves = [rows[pl.ds(2 * pair + half, R, stride=BCAP), :] for half in range(2)]
        far = jnp.concatenate(halves, axis=0).T
        cols = slice(pair * 128, (pair + 1) * 128)
        slot = 2 * pair + lax.broadcasted_iota(jnp.int32, (U, 128), 1) // R
        out_ref[:, cols] = jnp.where(slot < count[0], far + near_ref[:, cols], 0.0).astype(BF16)


VM = pl.BlockSpec(memory_space=pltpu.VMEM)
SM = pl.BlockSpec(memory_space=pltpu.SMEM)


def per_device(
    sources,
    live_counts,
    aggregate,
    translators,
    boundary_lists,
    far_sources,
    far_translators,
    near_blocks,
    near_columns,
):
    dir_index = lax.axis_index("dir")
    counts = live_counts[0]
    own_count = lax.dynamic_slice(counts, (dir_index,), (1,))
    slot_ids = jnp.arange(S_CL, dtype=jnp.int32)
    live = (slot_ids % BCAP < jnp.repeat(counts, BCAP)).astype(jnp.int32)

    send = pl.pallas_call(
        deal_kernel,
        out_shape=jax.ShapeDtypeStruct((N_DIR, 2 * RD * BCAP, 128), BF16),
        in_specs=[VM, VM],
        out_specs=VM,
        scratch_shapes=[pltpu.VMEM((R * BCAP, 128), F32), pltpu.VMEM((KD, 384), F32)],
        name="deal",
    )(sources, translators.T)
    recv = lax.all_to_all(send, "dir", split_axis=0, concat_axis=0, tiled=True)
    agg = jnp.pad(aggregate.T, ((0, 128 - U), (0, 0)))

    up, down = pl.pallas_call(
        boundary_kernel,
        out_shape=[jax.ShapeDtypeStruct((RD, NBND, 128), BF16)] * 2,
        in_specs=[VM, VM, VM],
        out_specs=[VM, VM],
        name="boundary",
    )(recv, boundary_lists.reshape(2 * NBND, 1), live.reshape(1, S_CL))
    before = shifted(up, "clus", 1)
    after = shifted(down, "clus", -1)

    near = pl.pallas_call(
        near_kernel,
        out_shape=jax.ShapeDtypeStruct((U, BCAP * R), F32),
        in_specs=[SM, SM, VM, VM],
        out_specs=VM,
        scratch_shapes=[pltpu.VMEM((BCAP, U, R), BF16), pltpu.VMEM((NN * U, R), BF16)],
        name="near",
    )(near_columns, own_count, sources, near_blocks)

    far = pl.pallas_call(
        far_kernel,
        out_shape=jax.ShapeDtypeStruct((N_DIR, RD, BCAP, U), BF16),
        in_specs=[SM, SM, SM, VM, VM, VM, VM, VM],
        out_specs=VM,
        scratch_shapes=[
            pltpu.VMEM((S_EXT * 16, 128), F32),
            pltpu.VMEM((NTR_PAD * 8, 128), F32),
            pltpu.VMEM((S_CL * 16, 128), F32),
        ],
        name="far",
    )(
        (far_translators * 8).reshape(-1),
        (far_sources * 16).reshape(-1),
        counts,
        recv,
        live.reshape(S_CL, 1),
        before,
        after,
        agg,
    )
    back = lax.all_to_all(far, "dir", split_axis=0, concat_axis=0, tiled=True)

    return pl.pallas_call(
        finish_kernel,
        out_shape=jax.ShapeDtypeStruct((U, BCAP * R), BF16),
        in_specs=[SM, VM, VM],
        out_specs=VM,
        scratch_shapes=[pltpu.VMEM((R * BCAP, U), F32)],
        name="finish",
    )(own_count, back, near)


def solution(mesh):
    in_specs = (
        P(None, ("clus", "dir")),
        P("clus", None),
        P(),
        P(None, "dir"),
        P("clus", None, None),
        P("clus", None),
        P("clus", None),
        P(("clus", "dir"), None, None),
        P(("clus", "dir"), None),
    )
    out_specs = P(None, ("clus", "dir"))
    return jax.shard_map(
        per_device, mesh=mesh, in_specs=in_specs, out_specs=out_specs, check_vma=False
    )
```

```python
import jax
import jax.numpy as jnp
from jax import lax
from jax.experimental import pallas as pl
from jax.experimental.pallas import tpu as pltpu
from jax.sharding import PartitionSpec as P

U = 96
K = 512
R = 64
NTR = 316
NI = 128
NN = 6
NBND = 32
BCAP = 16
S_CL = 256
S_EXT = 320
N_DIR = 16
KD = K // N_DIR
RD = R // N_DIR
KC = K // 128
NTR_PAD = 320
NHALF = NTR_PAD // 2
LAST = (S_CL - 1) * NI + 1
F32 = jnp.float32
BF16 = jnp.bfloat16


def shifted(value, axis, steps):
    count = lax.axis_size(axis)
    leading, last = (max(0, -steps), min(count, count - steps))
    return lax.ppermute(value, axis, [(source, source + steps) for source in range(leading, last)])


def deal_kernel(src_ref, kinds_ref, out_ref, rows, wide):
    for pair in range(BCAP // 2):
        both = src_ref[:, pair * 128 : (pair + 1) * 128].astype(F32)
        both = jnp.concatenate([both, jnp.zeros((128 - U, 128), F32)], axis=0).T
        for half in range(2):
            rows[pl.ds(2 * pair + half, R, stride=BCAP), :] = both[half * R : (half + 1) * R]
    wide[...] = jnp.zeros_like(wide)
    wide[:, :NTR] = kinds_ref[...].astype(F32)
    upper = lax.axis_index("clus") % 2 == 1
    low, mid, high = (wide[:, c * 128 : (c + 1) * 128] for c in range(3))
    lane = lax.broadcasted_iota(jnp.int32, (KD, 128), 1)
    shifted_up = jnp.where(lane < U, pltpu.roll(mid, U, 1), pltpu.roll(high, U, 1))
    tail = jnp.where(upper, shifted_up, low).astype(BF16)
    spare = jnp.where(upper, pltpu.roll(high, U - KD, 1), pltpu.roll(mid, U, 1))
    for d in range(N_DIR):
        first = d * RD * BCAP
        block = jnp.where(lane < U, rows[first : first + KD, :], spare)
        out_ref[d, :KD] = block.astype(BF16)
        out_ref[d, KD : RD * BCAP] = rows[first + KD : first + RD * BCAP, :].astype(BF16)
        out_ref[d, RD * BCAP :] = tail


def units_of(recv_ref, r):
    return recv_ref[:, r * BCAP : (r + 1) * BCAP].reshape(S_CL, 128)


def boundary_kernel(recv_ref, list_ref, live_ref, up_ref, down_ref, kinds_ref):
    for first, count, lane, row in ((0, 128, 0, RD * BCAP), (128, 32, U, 0)):
        pick = lax.broadcasted_iota(jnp.int32, (count, 128), 0) + lane == lax.broadcasted_iota(
            jnp.int32, (count, 128), 1
        )
        turned = lax.dot_general(
            pick.astype(F32).astype(BF16),
            recv_ref[:, row : row + KD].reshape(K, 128),
            (((1,), (1,)), ((), ())),
            preferred_element_type=F32,
        )
        kinds_ref[first : first + count, :] = turned.astype(BF16)
    slots = lax.broadcasted_iota(jnp.int32, (2 * NBND, S_CL), 1)
    pick = ((slots == list_ref[...]) & (live_ref[...] > 0)).astype(F32).astype(BF16)
    for r in range(RD):
        chosen = jnp.dot(pick, units_of(recv_ref, r), preferred_element_type=F32).astype(BF16)
        up_ref[r] = chosen[:NBND]
        down_ref[r] = chosen[NBND:]


def far_kernel(
    counts,
    kinds_hbm,
    sources_hbm,
    recv_ref,
    live_ref,
    before_ref,
    after_ref,
    agg_ref,
    mine_ref,
    other_ref,
    out_ref,
    ext,
    table,
    incoming,
    kind_rows,
    source_rows,
    sems,
):
    copies = []
    for d in range(N_DIR):
        part = pl.ds(d * BCAP * NI, BCAP * NI)
        copies.append(
            (
                pltpu.make_async_copy(kinds_hbm.at[part], kind_rows.at[part], sems.at[d, 0]),
                pltpu.make_async_copy(sources_hbm.at[part], source_rows.at[part], sems.at[d, 1]),
            )
        )
        for copy in copies[d]:
            copy.start()
    agg = agg_ref[...]
    for r in range(RD):
        own = jnp.dot(units_of(recv_ref, r), agg, preferred_element_type=F32)
        own = jnp.where(live_ref[...] > 0, own, 0.0)
        prev = jnp.dot(before_ref[r], agg, preferred_element_type=F32)
        foll = jnp.dot(after_ref[r], agg, preferred_element_type=F32)
        for c in range(KC):
            lanes = slice(c * 128, (c + 1) * 128)
            at = r * KC + c
            ext[pl.ds(at, S_CL, stride=16), :] = own[:, lanes]
            ext[pl.ds(S_CL * 16 + at, NBND, stride=16), :] = prev[:, lanes]
            ext[pl.ds((S_CL + NBND) * 16 + at, NBND, stride=16), :] = foll[:, lanes]
    upper = lax.axis_index("clus") % 2 == 1
    mine, other = mine_ref[...].astype(F32), other_ref[...].astype(F32)
    for first, kinds in ((0, jnp.where(upper, other, mine)), (NHALF, jnp.where(upper, mine, other))):
        for c in range(KC):
            part = kinds[:, c * 128 : (c + 1) * 128]
            table[pl.ds(first * 8 + c, NHALF, stride=8), :] = part
            table[pl.ds(first * 8 + c + KC, NHALF, stride=8), :] = part
    incoming[...] = jnp.zeros_like(incoming)

    def device(d, carry):
        part = pl.ds(d * BCAP * NI, BCAP * NI)
        pltpu.make_async_copy(kinds_hbm.at[part], kind_rows.at[part], sems.at[d, 0]).wait()
        pltpu.make_async_copy(sources_hbm.at[part], source_rows.at[part], sems.at[d, 1]).wait()

        def target(j, inner):
            t = d * BCAP + j
            first = t * NI
            sums = [[jnp.zeros((8, 128), F32) for _ in range(2)] for _ in range(2)]
            for i in range(NI):
                n8 = pl.multiple_of(kind_rows.at[pl.ds(i, LAST)][first], 8)
                s16 = pl.multiple_of(source_rows.at[pl.ds(i, LAST)][first], 16)
                weight = table[pl.ds(n8, 8), :]
                for h in range(2):
                    sums[i % 2][h] = sums[i % 2][h] + weight * ext[pl.ds(s16 + 8 * h, 8), :]
            for h in range(2):
                incoming[pl.ds(pl.multiple_of(t * 16 + 8 * h, 8), 8), :] = sums[0][h] + sums[1][h]
            return inner

        return lax.fori_loop(0, counts[d], target, carry)

    lax.fori_loop(0, N_DIR, device, 0)
    for r in range(RD):
        far = jnp.zeros((S_CL, U), F32)
        for c in range(KC):
            part = incoming[pl.ds(r * KC + c, S_CL, stride=16), :].astype(BF16)
            far = far + lax.dot_general(
                part,
                agg[:U, c * 128 : (c + 1) * 128],
                (((1,), (1,)), ((), ())),
                preferred_element_type=F32,
            )
        out_ref[:, r] = far.reshape(N_DIR, BCAP, U).astype(BF16)


def near_kernel(columns, count, src_ref, blocks_ref, out_ref, units, stack):
    for pair in range(BCAP // 2):
        both = src_ref[:, pair * 128 : (pair + 1) * 128].astype(F32)
        for half in range(2):
            slot = 2 * pair + half
            own = both[:, half * R : (half + 1) * R]
            units[slot] = jnp.where(count[0] > slot, own, 0.0).astype(BF16)
    for pair in range(BCAP // 2):
        halves = []
        for half in range(2):
            slot = 2 * pair + half
            for j in range(NN):
                stack[j * U : (j + 1) * U, :] = units[columns[slot, j]]
            halves.append(jnp.dot(blocks_ref[slot], stack[...], preferred_element_type=F32))
        out_ref[:, pair * 128 : (pair + 1) * 128] = jnp.concatenate(halves, axis=1)


def finish_kernel(count, back_ref, near_ref, out_ref, rows):
    rows[...] = back_ref[...].astype(F32).reshape(R * BCAP, U)
    for pair in range(BCAP // 2):
        halves = [rows[pl.ds(2 * pair + half, R, stride=BCAP), :] for half in range(2)]
        far = jnp.concatenate(halves, axis=0).T
        cols = slice(pair * 128, (pair + 1) * 128)
        slot = 2 * pair + lax.broadcasted_iota(jnp.int32, (U, 128), 1) // R
        out_ref[:, cols] = jnp.where(slot < count[0], far + near_ref[:, cols], 0.0).astype(BF16)


VM = pl.BlockSpec(memory_space=pltpu.VMEM)
SM = pl.BlockSpec(memory_space=pltpu.SMEM)
ANY = pl.BlockSpec(memory_space=pl.ANY)


def per_device(
    sources,
    live_counts,
    aggregate,
    translators,
    boundary_lists,
    far_sources,
    far_translators,
    near_blocks,
    near_columns,
):
    dir_index = lax.axis_index("dir")
    counts = live_counts[0]
    own_count = lax.dynamic_slice(counts, (dir_index,), (1,))
    slot_ids = jnp.arange(S_CL, dtype=jnp.int32)
    live = (slot_ids % BCAP < jnp.repeat(counts, BCAP)).astype(jnp.int32)

    send = pl.pallas_call(
        deal_kernel,
        out_shape=jax.ShapeDtypeStruct((N_DIR, RD * BCAP + KD, 128), BF16),
        in_specs=[VM, VM],
        out_specs=VM,
        scratch_shapes=[pltpu.VMEM((R * BCAP, 128), F32), pltpu.VMEM((KD, 384), F32)],
        name="deal",
    )(sources, translators.T)
    recv = lax.all_to_all(send, "dir", split_axis=0, concat_axis=0, tiled=True)
    agg = jnp.pad(aggregate.T, ((0, 128 - U), (0, 0)))

    up, down, mine = pl.pallas_call(
        boundary_kernel,
        out_shape=[jax.ShapeDtypeStruct((RD, NBND, 128), BF16)] * 2
        + [jax.ShapeDtypeStruct((NHALF, K), BF16)],
        in_specs=[VM, VM, VM],
        out_specs=[VM, VM, VM],
        name="boundary",
    )(recv, boundary_lists.reshape(2 * NBND, 1), live.reshape(1, S_CL))
    before = shifted(up, "clus", 1)
    after = shifted(down, "clus", -1)
    other = lax.ppermute(mine, "clus", [(c, c ^ 1) for c in range(lax.axis_size("clus"))])

    near = pl.pallas_call(
        near_kernel,
        out_shape=jax.ShapeDtypeStruct((U, BCAP * R), F32),
        in_specs=[SM, SM, VM, VM],
        out_specs=VM,
        scratch_shapes=[pltpu.VMEM((BCAP, U, R), BF16), pltpu.VMEM((NN * U, R), BF16)],
        name="near",
    )(near_columns, own_count, sources, near_blocks)

    far = pl.pallas_call(
        far_kernel,
        out_shape=jax.ShapeDtypeStruct((N_DIR, RD, BCAP, U), BF16),
        in_specs=[SM, ANY, ANY, VM, VM, VM, VM, VM, VM, VM],
        out_specs=VM,
        scratch_shapes=[
            pltpu.VMEM((S_EXT * 16, 128), F32),
            pltpu.VMEM((NTR_PAD * 8, 128), F32),
            pltpu.VMEM((S_CL * 16, 128), F32),
            pltpu.SMEM((S_CL * NI,), jnp.int32),
            pltpu.SMEM((S_CL * NI,), jnp.int32),
            pltpu.SemaphoreType.DMA((N_DIR, 2)),
        ],
        name="far",
    )(
        counts,
        (far_translators * 8).reshape(-1),
        (far_sources * 16).reshape(-1),
        recv,
        live.reshape(S_CL, 1),
        before,
        after,
        agg,
        mine,
        other,
    )
    back = lax.all_to_all(far, "dir", split_axis=0, concat_axis=0, tiled=True)

    return pl.pallas_call(
        finish_kernel,
        out_shape=jax.ShapeDtypeStruct((U, BCAP * R), BF16),
        in_specs=[SM, VM, VM],
        out_specs=VM,
        scratch_shapes=[pltpu.VMEM((R * BCAP, U), F32)],
        name="finish",
    )(own_count, back, near)


def solution(mesh):
    in_specs = (
        P(None, ("clus", "dir")),
        P("clus", None),
        P(),
        P(None, "dir"),
        P("clus", None, None),
        P("clus", None),
        P("clus", None),
        P(("clus", "dir"), None, None),
        P(("clus", "dir"), None),
    )
    out_specs = P(None, ("clus", "dir"))
    return jax.shard_map(
        per_device, mesh=mesh, in_specs=in_specs, out_specs=out_specs, check_vma=False
    )
```

```python
import jax
import jax.numpy as jnp
from jax import lax
from jax.experimental import pallas as pl
from jax.experimental.pallas import tpu as pltpu
from jax.sharding import PartitionSpec as P

U = 96
K = 512
R = 64
NTR = 316
NI = 128
NN = 6
NBND = 32
BCAP = 16
S_CL = 256
S_EXT = 320
N_DIR = 16
KD = K // N_DIR
RD = R // N_DIR
KC = K // 128
NTR_PAD = 320
NHALF = NTR_PAD // 2
STEP = 8
LAST = (S_CL - 1) * NI + 1
F32 = jnp.float32
BF16 = jnp.bfloat16


def deal_kernel(src_ref, kinds_ref, out_ref, rows, wide):
    for pair in range(BCAP // 2):
        both = src_ref[:, pair * 128 : (pair + 1) * 128].astype(F32)
        both = jnp.concatenate([both, jnp.zeros((128 - U, 128), F32)], axis=0).T
        for half in range(2):
            rows[pl.ds(2 * pair + half, R, stride=BCAP), :] = both[half * R : (half + 1) * R]
    wide[...] = jnp.zeros_like(wide)
    wide[:, :NTR] = kinds_ref[...].astype(F32)
    upper = lax.axis_index("clus") % 2 == 1
    low, mid, high = (wide[:, c * 128 : (c + 1) * 128] for c in range(3))
    lane = lax.broadcasted_iota(jnp.int32, (KD, 128), 1)
    shifted_up = jnp.where(lane < U, pltpu.roll(mid, U, 1), pltpu.roll(high, U, 1))
    tail = jnp.where(upper, shifted_up, low).astype(BF16)
    spare = jnp.where(upper, pltpu.roll(high, U - KD, 1), pltpu.roll(mid, U, 1))
    for d in range(N_DIR):
        first = d * RD * BCAP
        block = jnp.where(lane < U, rows[first : first + KD, :], spare)
        out_ref[d, :KD] = block.astype(BF16)
        out_ref[d, KD : RD * BCAP] = rows[first + KD : first + RD * BCAP, :].astype(BF16)
        out_ref[d, RD * BCAP :] = tail


def units_of(recv_ref, r):
    return recv_ref[:, r * BCAP : (r + 1) * BCAP].reshape(S_CL, 128)


def pack_kernel(counts, src_ref, kind_ref, packed_kinds, packed_sources, groups_ref, spots, values, moved):
    src, kind = src_ref[...], kind_ref[...]
    limit = jnp.full_like(src, BCAP)
    for d in range(N_DIR):
        limit = jnp.where(src // BCAP == d, counts[d], limit)
    live = src % BCAP < limit
    flags = live.astype(F32).astype(BF16)
    order = lax.broadcasted_iota(jnp.int32, (NI, NI), 0) <= lax.broadcasted_iota(jnp.int32, (NI, NI), 1)
    rank = jnp.dot(flags, order.astype(F32).astype(BF16), preferred_element_type=F32)
    spots[...] = jnp.where(live, rank - 1.0, -1.0).astype(jnp.int32)
    total = lax.dot_general(
        jnp.ones((8, NI), BF16), flags, (((1,), (1,)), ((), ())), preferred_element_type=F32
    )
    groups_ref[...] = (total.astype(jnp.int32) + STEP - 1) // STEP
    back = S_EXT - src
    for q, part in enumerate((back // 16 * 16, back % 16, kind // 16 * 16, kind % 16)):
        values[pl.ds(q, S_CL, stride=8), :] = part.astype(F32)
        values[pl.ds(q + 4, S_CL, stride=8), :] = jnp.zeros((S_CL, NI), F32)

    def eight(g, carry):
        rows = spots[pl.ds(pl.multiple_of(g * 8, 8), 8), :]
        for j in range(8):
            at = pl.ds(pl.multiple_of(g * 64, 64) + 8 * j, 8)
            place = lax.broadcasted_iota(jnp.int32, (NI, NI), 0) == rows[j : j + 1, :]
            moved[at, :] = lax.dot_general(
                values[at, :].astype(BF16),
                place.astype(F32).astype(BF16),
                (((1,), (1,)), ((), ())),
                preferred_element_type=F32,
            )
        return carry

    lax.fori_loop(0, S_CL // 8, eight, 0)
    parts = [moved[pl.ds(q, S_CL, stride=8), :].astype(jnp.int32) for q in range(4)]
    packed_sources[...] = (S_EXT - parts[0] - parts[1]) * 16
    packed_kinds[...] = (parts[2] + parts[3]) * 8


def boundary_kernel(recv_ref, list_ref, live_ref, inner_ref, outer_ref):
    upper = lax.axis_index("clus") % 2 == 1
    for first, count, lane, row in ((0, 128, 0, RD * BCAP), (128, 32, U, 0)):
        pick = lax.broadcasted_iota(jnp.int32, (count, 128), 0) + lane == lax.broadcasted_iota(
            jnp.int32, (count, 128), 1
        )
        turned = lax.dot_general(
            pick.astype(F32).astype(BF16),
            recv_ref[:, row : row + KD].reshape(K, 128),
            (((1,), (1,)), ((), ())),
            preferred_element_type=F32,
        ).astype(BF16)
        for c in range(KC):
            at = RD * NBND + c * NHALF + first
            inner_ref[at : at + count, :] = turned[:, c * 128 : (c + 1) * 128]
    slots = lax.broadcasted_iota(jnp.int32, (2 * NBND, S_CL), 1)
    pick = ((slots == list_ref[...]) & (live_ref[...] > 0)).astype(F32).astype(BF16)
    for r in range(RD):
        chosen = jnp.dot(pick, units_of(recv_ref, r), preferred_element_type=F32)
        up, down = chosen[:NBND], chosen[NBND:]
        rows = slice(r * NBND, (r + 1) * NBND)
        inner_ref[rows, :] = jnp.where(upper, down, up).astype(BF16)
        outer_ref[rows, :] = jnp.where(upper, up, down).astype(BF16)


def far_kernel(
    counts,
    groups,
    kinds_hbm,
    sources_hbm,
    recv_ref,
    live_ref,
    sent_ref,
    inner_ref,
    outer_ref,
    agg_ref,
    out_ref,
    ext,
    table,
    incoming,
    kind_rows,
    source_rows,
    sems,
):
    copies = []
    for d in range(N_DIR):
        part = pl.ds(d * BCAP * NI, BCAP * NI)
        copies.append(
            (
                pltpu.make_async_copy(kinds_hbm.at[part], kind_rows.at[part], sems.at[d, 0]),
                pltpu.make_async_copy(sources_hbm.at[part], source_rows.at[part], sems.at[d, 1]),
            )
        )
        for copy in copies[d]:
            copy.start()
    upper = lax.axis_index("clus") % 2 == 1
    agg = agg_ref[...]
    for r in range(RD):
        own = jnp.dot(units_of(recv_ref, r), agg, preferred_element_type=F32)
        own = jnp.where(live_ref[...] > 0, own, 0.0)
        rows = slice(r * NBND, (r + 1) * NBND)
        inner = jnp.dot(inner_ref[rows, :], agg, preferred_element_type=F32)
        outer = jnp.dot(outer_ref[rows, :], agg, preferred_element_type=F32)
        prev, foll = jnp.where(upper, inner, outer), jnp.where(upper, outer, inner)
        for c in range(KC):
            lanes = slice(c * 128, (c + 1) * 128)
            at = r * KC + c
            ext[pl.ds(at, S_CL, stride=16), :] = own[:, lanes]
            ext[pl.ds(S_CL * 16 + at, NBND, stride=16), :] = prev[:, lanes]
            ext[pl.ds((S_CL + NBND) * 16 + at, NBND, stride=16), :] = foll[:, lanes]
    ext[S_EXT * 16 :, :] = jnp.zeros((16, 128), F32)
    for c in range(KC):
        rows = slice(RD * NBND + c * NHALF, RD * NBND + (c + 1) * NHALF)
        mine, other = sent_ref[rows, :].astype(F32), inner_ref[rows, :].astype(F32)
        for first, part in ((0, jnp.where(upper, other, mine)), (NHALF, jnp.where(upper, mine, other))):
            table[pl.ds(first * 8 + c, NHALF, stride=8), :] = part
            table[pl.ds(first * 8 + c + KC, NHALF, stride=8), :] = part
    incoming[...] = jnp.zeros_like(incoming)

    def device(d, carry):
        part = pl.ds(d * BCAP * NI, BCAP * NI)
        pltpu.make_async_copy(kinds_hbm.at[part], kind_rows.at[part], sems.at[d, 0]).wait()
        pltpu.make_async_copy(sources_hbm.at[part], source_rows.at[part], sems.at[d, 1]).wait()

        def target(j, inner):
            t = d * BCAP + j
            first = t * NI
            group = groups[0, t]

            def run(count):
                sums = [[jnp.zeros((8, 128), F32) for _ in range(2)] for _ in range(2)]
                for i in range(count):
                    n8 = pl.multiple_of(kind_rows.at[pl.ds(i, LAST)][first], 8)
                    s16 = pl.multiple_of(source_rows.at[pl.ds(i, LAST)][first], 16)
                    weight = table[pl.ds(n8, 8), :]
                    for h in range(2):
                        sums[i % 2][h] = sums[i % 2][h] + weight * ext[pl.ds(s16 + 8 * h, 8), :]
                for h in range(2):
                    incoming[pl.ds(pl.multiple_of(t * 16 + 8 * h, 8), 8), :] = sums[0][h] + sums[1][h]

            def branch(low, high):
                if low == high:
                    run(low * STEP)
                    return
                mid = (low + high) // 2
                pl.when(group <= mid)(lambda: branch(low, mid))
                pl.when(group > mid)(lambda: branch(mid + 1, high))

            branch(0, NI // STEP)
            return inner

        return lax.fori_loop(0, counts[d], target, carry)

    lax.fori_loop(0, N_DIR, device, 0)
    for r in range(RD):
        far = jnp.zeros((S_CL, U), F32)
        for c in range(KC):
            part = incoming[pl.ds(r * KC + c, S_CL, stride=16), :].astype(BF16)
            far = far + lax.dot_general(
                part,
                agg[:U, c * 128 : (c + 1) * 128],
                (((1,), (1,)), ((), ())),
                preferred_element_type=F32,
            )
        out_ref[:, r] = far.reshape(N_DIR, BCAP, U).astype(BF16)


def near_kernel(columns, count, src_ref, blocks_ref, out_ref, units, stack):
    for pair in range(BCAP // 2):
        both = src_ref[:, pair * 128 : (pair + 1) * 128].astype(F32)
        for half in range(2):
            slot = 2 * pair + half
            own = both[:, half * R : (half + 1) * R]
            units[slot] = jnp.where(count[0] > slot, own, 0.0).astype(BF16)
    for pair in range(BCAP // 2):
        halves = []
        for half in range(2):
            slot = 2 * pair + half
            for j in range(NN):
                stack[j * U : (j + 1) * U, :] = units[columns[slot, j]]
            halves.append(jnp.dot(blocks_ref[slot], stack[...], preferred_element_type=F32))
        out_ref[:, pair * 128 : (pair + 1) * 128] = jnp.concatenate(halves, axis=1)


def finish_kernel(count, back_ref, near_ref, out_ref, rows):
    rows[...] = back_ref[...].astype(F32).reshape(R * BCAP, U)
    for pair in range(BCAP // 2):
        halves = [rows[pl.ds(2 * pair + half, R, stride=BCAP), :] for half in range(2)]
        far = jnp.concatenate(halves, axis=0).T
        cols = slice(pair * 128, (pair + 1) * 128)
        slot = 2 * pair + lax.broadcasted_iota(jnp.int32, (U, 128), 1) // R
        out_ref[:, cols] = jnp.where(slot < count[0], far + near_ref[:, cols], 0.0).astype(BF16)


VM = pl.BlockSpec(memory_space=pltpu.VMEM)
SM = pl.BlockSpec(memory_space=pltpu.SMEM)
ANY = pl.BlockSpec(memory_space=pl.ANY)


def per_device(
    sources,
    live_counts,
    aggregate,
    translators,
    boundary_lists,
    far_sources,
    far_translators,
    near_blocks,
    near_columns,
):
    dir_index = lax.axis_index("dir")
    counts = live_counts[0]
    own_count = lax.dynamic_slice(counts, (dir_index,), (1,))
    slot_ids = jnp.arange(S_CL, dtype=jnp.int32)
    live = (slot_ids % BCAP < jnp.repeat(counts, BCAP)).astype(jnp.int32)

    send = pl.pallas_call(
        deal_kernel,
        out_shape=jax.ShapeDtypeStruct((N_DIR, RD * BCAP + KD, 128), BF16),
        in_specs=[VM, VM],
        out_specs=VM,
        scratch_shapes=[pltpu.VMEM((R * BCAP, 128), F32), pltpu.VMEM((KD, 384), F32)],
        name="deal",
    )(sources, translators.T)
    recv = lax.all_to_all(send, "dir", split_axis=0, concat_axis=0, tiled=True)
    recv = pltpu.with_memory_space_constraint(recv, pltpu.VMEM)
    agg = jnp.pad(aggregate.T, ((0, 128 - U), (0, 0)))

    sent, edge = pl.pallas_call(
        boundary_kernel,
        out_shape=[
            jax.ShapeDtypeStruct((RD * NBND + KC * NHALF, 128), BF16),
            jax.ShapeDtypeStruct((RD * NBND, 128), BF16),
        ],
        in_specs=[VM, VM, VM],
        out_specs=[VM, VM],
        name="boundary",
    )(recv, boundary_lists.reshape(2 * NBND, 1), live.reshape(1, S_CL))
    clusters = lax.axis_size("clus")
    inner = lax.ppermute(sent, "clus", [(c, c ^ 1) for c in range(clusters)])
    outer = lax.ppermute(edge, "clus", [(c, (c ^ 1) + 2 * (2 * (c % 2) - 1)) for c in range(1, clusters - 1)])
    inner, outer = (pltpu.with_memory_space_constraint(x, pltpu.VMEM) for x in (inner, outer))

    near = pl.pallas_call(
        near_kernel,
        out_shape=jax.ShapeDtypeStruct((U, BCAP * R), F32),
        in_specs=[SM, SM, VM, VM],
        out_specs=VM,
        scratch_shapes=[pltpu.VMEM((BCAP, U, R), BF16), pltpu.VMEM((NN * U, R), BF16)],
        name="near",
    )(near_columns, own_count, sources, near_blocks)

    kind_rows, source_rows, groups = pl.pallas_call(
        pack_kernel,
        out_shape=[jax.ShapeDtypeStruct((S_CL, NI), jnp.int32)] * 2
        + [jax.ShapeDtypeStruct((8, S_CL), jnp.int32)],
        in_specs=[SM, VM, VM],
        out_specs=[VM, VM, VM],
        scratch_shapes=[
            pltpu.VMEM((S_CL, NI), jnp.int32),
            pltpu.VMEM((S_CL * 8, NI), F32),
            pltpu.VMEM((S_CL * 8, NI), F32),
        ],
        name="pack",
    )(counts, far_sources, far_translators)
    far = pl.pallas_call(
        far_kernel,
        out_shape=jax.ShapeDtypeStruct((N_DIR, RD, BCAP, U), BF16),
        in_specs=[SM, SM, ANY, ANY, VM, VM, VM, VM, VM, VM],
        out_specs=VM,
        scratch_shapes=[
            pltpu.VMEM(((S_EXT + 1) * 16, 128), F32),
            pltpu.VMEM((NTR_PAD * 8, 128), F32),
            pltpu.VMEM((S_CL * 16, 128), F32),
            pltpu.SMEM((S_CL * NI,), jnp.int32),
            pltpu.SMEM((S_CL * NI,), jnp.int32),
            pltpu.SemaphoreType.DMA((N_DIR, 2)),
        ],
        name="far",
    )(
        counts,
        groups,
        kind_rows.reshape(-1),
        source_rows.reshape(-1),
        recv,
        live.reshape(S_CL, 1),
        sent,
        inner,
        outer,
        agg,
    )
    back = lax.all_to_all(far, "dir", split_axis=0, concat_axis=0, tiled=True)
    back = pltpu.with_memory_space_constraint(back, pltpu.VMEM)

    return pl.pallas_call(
        finish_kernel,
        out_shape=jax.ShapeDtypeStruct((U, BCAP * R), BF16),
        in_specs=[SM, VM, VM],
        out_specs=VM,
        scratch_shapes=[pltpu.VMEM((R * BCAP, U), F32)],
        name="finish",
    )(own_count, back, near)


def solution(mesh):
    in_specs = (
        P(None, ("clus", "dir")),
        P("clus", None),
        P(),
        P(None, "dir"),
        P("clus", None, None),
        P("clus", None),
        P("clus", None),
        P(("clus", "dir"), None, None),
        P(("clus", "dir"), None),
    )
    out_specs = P(None, ("clus", "dir"))
    return jax.shard_map(
        per_device, mesh=mesh, in_specs=in_specs, out_specs=out_specs, check_vma=False
    )
```

```python
import jax
import jax.numpy as jnp
from jax import lax
from jax.experimental import pallas as pl
from jax.experimental.pallas import tpu as pltpu
from jax.sharding import PartitionSpec as P

U = 96
K = 512
R = 64
NTR = 316
NI = 128
NN = 6
NBND = 32
BCAP = 16
S_CL = 256
S_EXT = 320
N_DIR = 16
KD = K // N_DIR
RD = R // N_DIR
KC = K // 128
NTR_PAD = 320
NHALF = NTR_PAD // 2
STEP = 16
LAST = (S_CL - 1) * NI + 1
F32 = jnp.float32
BF16 = jnp.bfloat16


def deal_kernel(src_ref, kinds_ref, out_ref, rows, wide):
    for pair in range(BCAP // 2):
        both = src_ref[:, pair * 128 : (pair + 1) * 128].astype(F32)
        both = jnp.concatenate([both, jnp.zeros((128 - U, 128), F32)], axis=0).T
        for half in range(2):
            rows[pl.ds(2 * pair + half, R, stride=BCAP), :] = both[half * R : (half + 1) * R]
    wide[...] = jnp.zeros_like(wide)
    wide[:, :NTR] = kinds_ref[...].astype(F32)
    upper = lax.axis_index("clus") % 2 == 1
    low, mid, high = (wide[:, c * 128 : (c + 1) * 128] for c in range(3))
    lane = lax.broadcasted_iota(jnp.int32, (KD, 128), 1)
    shifted_up = jnp.where(lane < U, pltpu.roll(mid, U, 1), pltpu.roll(high, U, 1))
    tail = jnp.where(upper, shifted_up, low).astype(BF16)
    spare = jnp.where(upper, pltpu.roll(high, U - KD, 1), pltpu.roll(mid, U, 1))
    for d in range(N_DIR):
        first = d * RD * BCAP
        block = jnp.where(lane < U, rows[first : first + KD, :], spare)
        out_ref[d, :KD] = block.astype(BF16)
        out_ref[d, KD : RD * BCAP] = rows[first + KD : first + RD * BCAP, :].astype(BF16)
        out_ref[d, RD * BCAP :] = tail


def units_of(recv_ref, r):
    return recv_ref[:, r * BCAP : (r + 1) * BCAP].reshape(S_CL, 128)


def pack_kernel(counts, src_ref, kind_ref, packed_kinds, packed_sources, groups_ref, spots, values, moved):
    src, kind = src_ref[...], kind_ref[...]
    limit = jnp.full_like(src, BCAP)
    for d in range(N_DIR):
        limit = jnp.where(src // BCAP == d, counts[d], limit)
    live = src % BCAP < limit
    flags = live.astype(F32).astype(BF16)
    order = lax.broadcasted_iota(jnp.int32, (NI, NI), 0) <= lax.broadcasted_iota(jnp.int32, (NI, NI), 1)
    rank = jnp.dot(flags, order.astype(F32).astype(BF16), preferred_element_type=F32)
    spots[...] = jnp.where(live, rank - 1.0, -1.0).astype(jnp.int32)
    total = lax.dot_general(
        jnp.ones((8, NI), BF16), flags, (((1,), (1,)), ((), ())), preferred_element_type=F32
    )
    groups_ref[...] = (total.astype(jnp.int32) + STEP - 1) // STEP
    back = S_EXT - src
    for q, part in enumerate((back // 16 * 16, back % 16, kind // 16 * 16, kind % 16)):
        values[pl.ds(q, S_CL, stride=8), :] = part.astype(F32)
        values[pl.ds(q + 4, S_CL, stride=8), :] = jnp.zeros((S_CL, NI), F32)

    def eight(g, carry):
        rows = spots[pl.ds(pl.multiple_of(g * 8, 8), 8), :]
        for j in range(8):
            at = pl.ds(pl.multiple_of(g * 64, 64) + 8 * j, 8)
            place = lax.broadcasted_iota(jnp.int32, (NI, NI), 0) == rows[j : j + 1, :]
            moved[at, :] = lax.dot_general(
                values[at, :].astype(BF16),
                place.astype(F32).astype(BF16),
                (((1,), (1,)), ((), ())),
                preferred_element_type=F32,
            )
        return carry

    lax.fori_loop(0, S_CL // 8, eight, 0)
    parts = [moved[pl.ds(q, S_CL, stride=8), :].astype(jnp.int32) for q in range(4)]
    packed_sources[...] = (S_EXT - parts[0] - parts[1]) * 16
    packed_kinds[...] = (parts[2] + parts[3]) * 8


def boundary_kernel(recv_ref, list_ref, live_ref, _, inner_ref, outer_ref):
    upper = lax.axis_index("clus") % 2 == 1
    for first, count, lane, row in ((0, 128, 0, RD * BCAP), (128, 32, U, 0)):
        pick = lax.broadcasted_iota(jnp.int32, (count, 128), 0) + lane == lax.broadcasted_iota(
            jnp.int32, (count, 128), 1
        )
        turned = lax.dot_general(
            pick.astype(F32).astype(BF16),
            recv_ref[:, row : row + KD].reshape(K, 128),
            (((1,), (1,)), ((), ())),
            preferred_element_type=F32,
        ).astype(BF16)
        for c in range(KC):
            at = RD * NBND + c * NHALF + first
            inner_ref[at : at + count, :] = turned[:, c * 128 : (c + 1) * 128]
    slots = lax.broadcasted_iota(jnp.int32, (2 * NBND, S_CL), 1)
    pick = ((slots == list_ref[...]) & (live_ref[...] > 0)).astype(F32).astype(BF16)
    for r in range(RD):
        chosen = jnp.dot(pick, units_of(recv_ref, r), preferred_element_type=F32)
        up, down = chosen[:NBND], chosen[NBND:]
        rows = slice(r * NBND, (r + 1) * NBND)
        inner_ref[rows, :] = jnp.where(upper, down, up).astype(BF16)
        outer_ref[rows, :] = jnp.where(upper, up, down).astype(BF16)


def far_kernel(
    counts,
    groups,
    kinds_hbm,
    sources_hbm,
    recv_ref,
    live_ref,
    sent_ref,
    inner_ref,
    outer_ref,
    agg_ref,
    out_ref,
    ext,
    table,
    incoming,
    kind_rows,
    source_rows,
    sems,
):
    copies = []
    for d in range(N_DIR):
        part = pl.ds(d * BCAP * NI, BCAP * NI)
        copies.append(
            (
                pltpu.make_async_copy(kinds_hbm.at[part], kind_rows.at[part], sems.at[d, 0]),
                pltpu.make_async_copy(sources_hbm.at[part], source_rows.at[part], sems.at[d, 1]),
            )
        )
        for copy in copies[d]:
            copy.start()
    upper = lax.axis_index("clus") % 2 == 1
    agg = agg_ref[...]
    for r in range(RD):
        own = jnp.dot(units_of(recv_ref, r), agg, preferred_element_type=F32)
        own = jnp.where(live_ref[...] > 0, own, 0.0)
        rows = slice(r * NBND, (r + 1) * NBND)
        inner = jnp.dot(inner_ref[rows, :], agg, preferred_element_type=F32)
        outer = jnp.dot(outer_ref[rows, :], agg, preferred_element_type=F32)
        prev, foll = jnp.where(upper, inner, outer), jnp.where(upper, outer, inner)
        for c in range(KC):
            lanes = slice(c * 128, (c + 1) * 128)
            at = r * KC + c
            ext[pl.ds(at, S_CL, stride=16), :] = own[:, lanes]
            ext[pl.ds(S_CL * 16 + at, NBND, stride=16), :] = prev[:, lanes]
            ext[pl.ds((S_CL + NBND) * 16 + at, NBND, stride=16), :] = foll[:, lanes]
    ext[S_EXT * 16 :, :] = jnp.zeros((16, 128), F32)
    for c in range(KC):
        rows = slice(RD * NBND + c * NHALF, RD * NBND + (c + 1) * NHALF)
        mine, other = sent_ref[rows, :].astype(F32), inner_ref[rows, :].astype(F32)
        for first, part in ((0, jnp.where(upper, other, mine)), (NHALF, jnp.where(upper, mine, other))):
            table[pl.ds(first * 8 + c, NHALF, stride=8), :] = part
            table[pl.ds(first * 8 + c + KC, NHALF, stride=8), :] = part
    incoming[...] = jnp.zeros_like(incoming)

    def device(d, carry):
        part = pl.ds(d * BCAP * NI, BCAP * NI)
        pltpu.make_async_copy(kinds_hbm.at[part], kind_rows.at[part], sems.at[d, 0]).wait()
        pltpu.make_async_copy(sources_hbm.at[part], source_rows.at[part], sems.at[d, 1]).wait()

        def target(j, inner):
            t = d * BCAP + j
            first = t * NI
            group = groups[0, t]

            def run(count):
                sums = [[jnp.zeros((8, 128), F32) for _ in range(2)] for _ in range(2)]
                for i in range(count):
                    n8 = pl.multiple_of(kind_rows.at[pl.ds(i, LAST)][first], 8)
                    s16 = pl.multiple_of(source_rows.at[pl.ds(i, LAST)][first], 16)
                    weight = table[pl.ds(n8, 8), :]
                    for h in range(2):
                        sums[i % 2][h] = sums[i % 2][h] + weight * ext[pl.ds(s16 + 8 * h, 8), :]
                for h in range(2):
                    incoming[pl.ds(pl.multiple_of(t * 16 + 8 * h, 8), 8), :] = sums[0][h] + sums[1][h]

            def branch(low, high):
                if low == high:
                    run(low * STEP)
                    return
                mid = (low + high) // 2
                lax.cond(group <= mid, lambda: branch(low, mid), lambda: branch(mid + 1, high))

            branch(0, NI // STEP)
            return inner

        return lax.fori_loop(0, counts[d], target, carry)

    lax.fori_loop(0, N_DIR, device, 0)
    for r in range(RD - 1):
        spare = jnp.concatenate([jnp.zeros((U, K), BF16), agg[r * 32 : (r + 1) * 32]], axis=0)
        far = jnp.zeros((S_CL, 128), F32)
        for right, side in ((r, agg), (RD - 1, spare)):
            for c in range(KC):
                far = far + lax.dot_general(
                    incoming[pl.ds(right * KC + c, S_CL, stride=16), :].astype(BF16),
                    side[:, c * 128 : (c + 1) * 128],
                    (((1,), (1,)), ((), ())),
                    preferred_element_type=F32,
                )
        out_ref[:, r * BCAP : (r + 1) * BCAP] = far.reshape(N_DIR, BCAP, 128).astype(BF16)


def near_kernel(columns, count, src_ref, blocks_ref, out_ref, units, stack):
    for pair in range(BCAP // 2):
        both = src_ref[:, pair * 128 : (pair + 1) * 128].astype(F32)
        for half in range(2):
            slot = 2 * pair + half
            own = both[:, half * R : (half + 1) * R]
            units[slot] = jnp.where(count[0] > slot, own, 0.0).astype(BF16)
    for pair in range(BCAP // 2):
        halves = []
        for half in range(2):
            slot = 2 * pair + half
            for j in range(NN):
                stack[j * U : (j + 1) * U, :] = units[columns[slot, j]]
            halves.append(jnp.dot(blocks_ref[slot], stack[...], preferred_element_type=F32))
        out_ref[:, pair * 128 : (pair + 1) * 128] = jnp.concatenate(halves, axis=1)


def finish_kernel(count, back_ref, near_ref, out_ref, rows):
    lane = lax.broadcasted_iota(jnp.int32, (S_CL, 128), 1)
    last = jnp.zeros((S_CL, 128), F32)
    for r in range(RD):
        if r < RD - 1:
            part = back_ref[:, r * BCAP : (r + 1) * BCAP].reshape(S_CL, 128).astype(F32)
            last = jnp.where(lane // 32 == r, pltpu.roll(part, r * 32 + 32, 1), last)
        else:
            part = last
        for d in range(N_DIR):
            first = (d * RD + r) * BCAP
            rows[first : first + BCAP, :] = part[d * BCAP : (d + 1) * BCAP]
    for pair in range(BCAP // 2):
        halves = [rows[pl.ds(2 * pair + half, R, stride=BCAP), :] for half in range(2)]
        far = jnp.concatenate(halves, axis=0).T[:U]
        cols = slice(pair * 128, (pair + 1) * 128)
        slot = 2 * pair + lax.broadcasted_iota(jnp.int32, (U, 128), 1) // R
        out_ref[:, cols] = jnp.where(slot < count[0], far + near_ref[:, cols], 0.0).astype(BF16)


VM = pl.BlockSpec(memory_space=pltpu.VMEM)
SM = pl.BlockSpec(memory_space=pltpu.SMEM)
ANY = pl.BlockSpec(memory_space=pl.ANY)


def per_device(
    sources,
    live_counts,
    aggregate,
    translators,
    boundary_lists,
    far_sources,
    far_translators,
    near_blocks,
    near_columns,
):
    dir_index = lax.axis_index("dir")
    counts = live_counts[0]
    own_count = lax.dynamic_slice(counts, (dir_index,), (1,))
    slot_ids = jnp.arange(S_CL, dtype=jnp.int32)
    live = (slot_ids % BCAP < jnp.repeat(counts, BCAP)).astype(jnp.int32)

    send = pl.pallas_call(
        deal_kernel,
        out_shape=jax.ShapeDtypeStruct((N_DIR, RD * BCAP + KD, 128), BF16),
        in_specs=[VM, VM],
        out_specs=VM,
        scratch_shapes=[pltpu.VMEM((R * BCAP, 128), F32), pltpu.VMEM((KD, 384), F32)],
        name="deal",
    )(sources, translators.T)
    recv = lax.all_to_all(send, "dir", split_axis=0, concat_axis=0, tiled=True)
    recv = pltpu.with_memory_space_constraint(recv, pltpu.VMEM)
    agg = jnp.pad(aggregate.T, ((0, 128 - U), (0, 0)))

    kind_rows, source_rows, groups = pl.pallas_call(
        pack_kernel,
        out_shape=[jax.ShapeDtypeStruct((S_CL, NI), jnp.int32)] * 2
        + [jax.ShapeDtypeStruct((8, S_CL), jnp.int32)],
        in_specs=[SM, VM, VM],
        out_specs=[VM, VM, VM],
        scratch_shapes=[
            pltpu.VMEM((S_CL, NI), jnp.int32),
            pltpu.VMEM((S_CL * 8, NI), F32),
            pltpu.VMEM((S_CL * 8, NI), F32),
        ],
        name="pack",
    )(counts, far_sources, far_translators)
    sent, edge = pl.pallas_call(
        boundary_kernel,
        out_shape=[
            jax.ShapeDtypeStruct((RD * NBND + KC * NHALF, 128), BF16),
            jax.ShapeDtypeStruct((RD * NBND, 128), BF16),
        ],
        in_specs=[VM, VM, VM, ANY],
        out_specs=[VM, VM],
        name="boundary",
    )(recv, boundary_lists.reshape(2 * NBND, 1), live.reshape(1, S_CL), groups)
    clusters = lax.axis_size("clus")
    inner = lax.ppermute(sent, "clus", [(c, c ^ 1) for c in range(clusters)])
    outer = lax.ppermute(edge, "clus", [(c, (c ^ 1) + 2 * (2 * (c % 2) - 1)) for c in range(1, clusters - 1)])
    inner, outer = (pltpu.with_memory_space_constraint(x, pltpu.VMEM) for x in (inner, outer))

    near = pl.pallas_call(
        near_kernel,
        out_shape=jax.ShapeDtypeStruct((U, BCAP * R), F32),
        in_specs=[SM, SM, VM, VM],
        out_specs=VM,
        scratch_shapes=[pltpu.VMEM((BCAP, U, R), BF16), pltpu.VMEM((NN * U, R), BF16)],
        name="near",
    )(near_columns, own_count, sources, near_blocks)

    far = pl.pallas_call(
        far_kernel,
        out_shape=jax.ShapeDtypeStruct((N_DIR, (RD - 1) * BCAP, 128), BF16),
        in_specs=[SM, SM, ANY, ANY, VM, VM, VM, VM, VM, VM],
        out_specs=VM,
        scratch_shapes=[
            pltpu.VMEM(((S_EXT + 1) * 16, 128), F32),
            pltpu.VMEM((NTR_PAD * 8, 128), F32),
            pltpu.VMEM((S_CL * 16, 128), F32),
            pltpu.SMEM((S_CL * NI,), jnp.int32),
            pltpu.SMEM((S_CL * NI,), jnp.int32),
            pltpu.SemaphoreType.DMA((N_DIR, 2)),
        ],
        name="far",
    )(
        counts,
        groups,
        kind_rows.reshape(-1),
        source_rows.reshape(-1),
        recv,
        live.reshape(S_CL, 1),
        sent,
        inner,
        outer,
        agg,
    )
    back = lax.all_to_all(far, "dir", split_axis=0, concat_axis=0, tiled=True)
    back = pltpu.with_memory_space_constraint(back, pltpu.VMEM)

    return pl.pallas_call(
        finish_kernel,
        out_shape=jax.ShapeDtypeStruct((U, BCAP * R), BF16),
        in_specs=[SM, VM, VM],
        out_specs=VM,
        scratch_shapes=[pltpu.VMEM((R * BCAP, 128), F32)],
        name="finish",
    )(own_count, back, near)


def solution(mesh):
    in_specs = (
        P(None, ("clus", "dir")),
        P("clus", None),
        P(),
        P(None, "dir"),
        P("clus", None, None),
        P("clus", None),
        P("clus", None),
        P(("clus", "dir"), None, None),
        P(("clus", "dir"), None),
    )
    out_specs = P(None, ("clus", "dir"))
    return jax.shard_map(
        per_device, mesh=mesh, in_specs=in_specs, out_specs=out_specs, check_vma=False
    )
```

```python
import jax
import jax.numpy as jnp
from jax import lax
from jax.experimental import pallas as pl
from jax.experimental.pallas import tpu as pltpu
from jax.sharding import PartitionSpec as P

U = 96
K = 512
R = 64
NTR = 316
NI = 128
NN = 6
NBND = 32
BCAP = 16
S_CL = 256
S_EXT = 320
N_DIR = 16
KD = K // N_DIR
RD = R // N_DIR
KC = K // 128
NTR_PAD = 320
NHALF = NTR_PAD // 2
STEP = 8
LAST = (S_CL - 1) * NI + 1
F32 = jnp.float32
BF16 = jnp.bfloat16


def deal_kernel(src_ref, kinds_ref, out_ref, rows, wide):
    for pair in range(BCAP // 2):
        both = src_ref[:, pair * 128 : (pair + 1) * 128].astype(F32)
        both = jnp.concatenate([both, jnp.zeros((128 - U, 128), F32)], axis=0).T
        for half in range(2):
            rows[pl.ds(2 * pair + half, R, stride=BCAP), :] = both[half * R : (half + 1) * R]
    wide[...] = jnp.zeros_like(wide)
    wide[:, :NTR] = kinds_ref[...].astype(F32)
    upper = lax.axis_index("clus") % 2 == 1
    low, mid, high = (wide[:, c * 128 : (c + 1) * 128] for c in range(3))
    lane = lax.broadcasted_iota(jnp.int32, (KD, 128), 1)
    shifted_up = jnp.where(lane < U, pltpu.roll(mid, U, 1), pltpu.roll(high, U, 1))
    tail = jnp.where(upper, shifted_up, low).astype(BF16)
    spare = jnp.where(upper, pltpu.roll(high, U - KD, 1), pltpu.roll(mid, U, 1))
    for d in range(N_DIR):
        first = d * RD * BCAP
        block = jnp.where(lane < U, rows[first : first + KD, :], spare)
        out_ref[d, :KD] = block.astype(BF16)
        out_ref[d, KD : RD * BCAP] = rows[first + KD : first + RD * BCAP, :].astype(BF16)
        out_ref[d, RD * BCAP :] = tail


def units_of(recv_ref, r):
    return recv_ref[:, r * BCAP : (r + 1) * BCAP].reshape(S_CL, 128)


def pack_kernel(counts, src_ref, kind_ref, packed_kinds, packed_sources, groups_ref, spots, values, moved):
    src, kind = src_ref[...], kind_ref[...]
    limit = jnp.full_like(src, BCAP)
    for d in range(N_DIR):
        limit = jnp.where(src // BCAP == d, counts[d], limit)
    live = src % BCAP < limit
    flags = live.astype(F32).astype(BF16)
    order = lax.broadcasted_iota(jnp.int32, (NI, NI), 0) <= lax.broadcasted_iota(jnp.int32, (NI, NI), 1)
    rank = jnp.dot(flags, order.astype(F32).astype(BF16), preferred_element_type=F32)
    spots[...] = jnp.where(live, rank - 1.0, -1.0).astype(jnp.int32)
    total = lax.dot_general(
        jnp.ones((8, NI), BF16), flags, (((1,), (1,)), ((), ())), preferred_element_type=F32
    )
    groups_ref[...] = (total.astype(jnp.int32) + STEP - 1) // STEP
    back = S_EXT - src
    for q, part in enumerate((back // 16 * 16, back % 16, kind // 16 * 16, kind % 16)):
        values[pl.ds(q, S_CL, stride=8), :] = part.astype(F32)
        values[pl.ds(q + 4, S_CL, stride=8), :] = jnp.zeros((S_CL, NI), F32)

    def eight(g, carry):
        rows = spots[pl.ds(pl.multiple_of(g * 8, 8), 8), :]
        for j in range(8):
            at = pl.ds(pl.multiple_of(g * 64, 64) + 8 * j, 8)
            place = lax.broadcasted_iota(jnp.int32, (NI, NI), 0) == rows[j : j + 1, :]
            moved[at, :] = lax.dot_general(
                values[at, :].astype(BF16),
                place.astype(F32).astype(BF16),
                (((1,), (1,)), ((), ())),
                preferred_element_type=F32,
            )
        return carry

    lax.fori_loop(0, S_CL // 8, eight, 0)
    parts = [moved[pl.ds(q, S_CL, stride=8), :].astype(jnp.int32) for q in range(4)]
    packed_sources[...] = (S_EXT - parts[0] - parts[1]) * 16
    packed_kinds[...] = (parts[2] + parts[3]) * 8


def boundary_kernel(recv_ref, list_ref, live_ref, _, inner_ref, outer_ref):
    upper = lax.axis_index("clus") % 2 == 1
    for first, count, lane, row in ((0, 128, 0, RD * BCAP), (128, 32, U, 0)):
        pick = lax.broadcasted_iota(jnp.int32, (count, 128), 0) + lane == lax.broadcasted_iota(
            jnp.int32, (count, 128), 1
        )
        turned = lax.dot_general(
            pick.astype(F32).astype(BF16),
            recv_ref[:, row : row + KD].reshape(K, 128),
            (((1,), (1,)), ((), ())),
            preferred_element_type=F32,
        ).astype(BF16)
        for c in range(KC):
            at = RD * NBND + c * NHALF + first
            inner_ref[at : at + count, :] = turned[:, c * 128 : (c + 1) * 128]
    slots = lax.broadcasted_iota(jnp.int32, (2 * NBND, S_CL), 1)
    pick = ((slots == list_ref[...]) & (live_ref[...] > 0)).astype(F32).astype(BF16)
    for r in range(RD):
        chosen = jnp.dot(pick, units_of(recv_ref, r), preferred_element_type=F32)
        up, down = chosen[:NBND], chosen[NBND:]
        rows = slice(r * NBND, (r + 1) * NBND)
        inner_ref[rows, :] = jnp.where(upper, down, up).astype(BF16)
        outer_ref[rows, :] = jnp.where(upper, up, down).astype(BF16)


def far_kernel(
    counts,
    groups,
    kinds_hbm,
    sources_hbm,
    recv_ref,
    live_ref,
    sent_ref,
    inner_ref,
    outer_ref,
    agg_ref,
    out_ref,
    ext,
    table,
    incoming,
    kind_rows,
    source_rows,
    sems,
):
    copies = []
    for d in range(N_DIR):
        part = pl.ds(d * BCAP * NI, BCAP * NI)
        copies.append(
            (
                pltpu.make_async_copy(kinds_hbm.at[part], kind_rows.at[part], sems.at[d, 0]),
                pltpu.make_async_copy(sources_hbm.at[part], source_rows.at[part], sems.at[d, 1]),
            )
        )
        for copy in copies[d]:
            copy.start()
    upper = lax.axis_index("clus") % 2 == 1
    agg = agg_ref[...]
    for r in range(RD):
        own = jnp.dot(units_of(recv_ref, r), agg, preferred_element_type=F32)
        own = jnp.where(live_ref[...] > 0, own, 0.0)
        rows = slice(r * NBND, (r + 1) * NBND)
        inner = jnp.dot(inner_ref[rows, :], agg, preferred_element_type=F32)
        outer = jnp.dot(outer_ref[rows, :], agg, preferred_element_type=F32)
        prev, foll = jnp.where(upper, inner, outer), jnp.where(upper, outer, inner)
        for c in range(KC):
            lanes = slice(c * 128, (c + 1) * 128)
            at = r * KC + c
            ext[pl.ds(at, S_CL, stride=16), :] = own[:, lanes]
            ext[pl.ds(S_CL * 16 + at, NBND, stride=16), :] = prev[:, lanes]
            ext[pl.ds((S_CL + NBND) * 16 + at, NBND, stride=16), :] = foll[:, lanes]
    ext[S_EXT * 16 :, :] = jnp.zeros((16, 128), F32)
    for c in range(KC):
        rows = slice(RD * NBND + c * NHALF, RD * NBND + (c + 1) * NHALF)
        mine, other = sent_ref[rows, :].astype(F32), inner_ref[rows, :].astype(F32)
        for first, part in ((0, jnp.where(upper, other, mine)), (NHALF, jnp.where(upper, mine, other))):
            table[pl.ds(first * 8 + c, NHALF, stride=8), :] = part
            table[pl.ds(first * 8 + c + KC, NHALF, stride=8), :] = part
    incoming[...] = jnp.zeros_like(incoming)

    def device(d, carry):
        part = pl.ds(d * BCAP * NI, BCAP * NI)
        pltpu.make_async_copy(kinds_hbm.at[part], kind_rows.at[part], sems.at[d, 0]).wait()
        pltpu.make_async_copy(sources_hbm.at[part], source_rows.at[part], sems.at[d, 1]).wait()

        def target(j, inner):
            t = d * BCAP + j
            first = t * NI
            group = groups[0, t]

            def run(count):
                sums = [[jnp.zeros((8, 128), F32) for _ in range(2)] for _ in range(2)]
                for i in range(count):
                    n8 = pl.multiple_of(kind_rows.at[pl.ds(i, LAST)][first], 8)
                    s16 = pl.multiple_of(source_rows.at[pl.ds(i, LAST)][first], 16)
                    weight = table[pl.ds(n8, 8), :]
                    for h in range(2):
                        sums[i % 2][h] = sums[i % 2][h] + weight * ext[pl.ds(s16 + 8 * h, 8), :]
                for h in range(2):
                    incoming[pl.ds(pl.multiple_of(t * 16 + 8 * h, 8), 8), :] = sums[0][h] + sums[1][h]

            def branch(low, high):
                if low == high:
                    run(low * STEP)
                    return
                mid = (low + high) // 2
                lax.cond(group <= mid, lambda: branch(low, mid), lambda: branch(mid + 1, high))

            branch(0, NI // STEP)
            return inner

        return lax.fori_loop(0, counts[d], target, carry)

    lax.fori_loop(0, N_DIR, device, 0)
    for r in range(RD - 1):
        spare = jnp.concatenate([jnp.zeros((U, K), BF16), agg[r * 32 : (r + 1) * 32]], axis=0)
        far = jnp.zeros((S_CL, 128), F32)
        for right, side in ((r, agg), (RD - 1, spare)):
            for c in range(KC):
                far = far + lax.dot_general(
                    incoming[pl.ds(right * KC + c, S_CL, stride=16), :].astype(BF16),
                    side[:, c * 128 : (c + 1) * 128],
                    (((1,), (1,)), ((), ())),
                    preferred_element_type=F32,
                )
        out_ref[:, r * BCAP : (r + 1) * BCAP] = far.reshape(N_DIR, BCAP, 128).astype(BF16)


def near_kernel(columns, count, src_ref, blocks_ref, out_ref, units, stack):
    for pair in range(BCAP // 2):
        both = src_ref[:, pair * 128 : (pair + 1) * 128].astype(F32)
        for half in range(2):
            slot = 2 * pair + half
            own = both[:, half * R : (half + 1) * R]
            units[slot] = jnp.where(count[0] > slot, own, 0.0).astype(BF16)
    for pair in range(BCAP // 2):
        halves = []
        for half in range(2):
            slot = 2 * pair + half
            for j in range(NN):
                stack[j * U : (j + 1) * U, :] = units[columns[slot, j]]
            halves.append(jnp.dot(blocks_ref[slot], stack[...], preferred_element_type=F32))
        out_ref[:, pair * 128 : (pair + 1) * 128] = jnp.concatenate(halves, axis=1)


def finish_kernel(count, back_ref, near_ref, out_ref, rows):
    lane = lax.broadcasted_iota(jnp.int32, (S_CL, 128), 1)
    last = jnp.zeros((S_CL, 128), F32)
    for r in range(RD):
        if r < RD - 1:
            part = back_ref[:, r * BCAP : (r + 1) * BCAP].reshape(S_CL, 128).astype(F32)
            last = jnp.where(lane // 32 == r, pltpu.roll(part, r * 32 + 32, 1), last)
        else:
            part = last
        for d in range(N_DIR):
            first = (d * RD + r) * BCAP
            rows[first : first + BCAP, :] = part[d * BCAP : (d + 1) * BCAP]
    for pair in range(BCAP // 2):
        halves = [rows[pl.ds(2 * pair + half, R, stride=BCAP), :] for half in range(2)]
        far = jnp.concatenate(halves, axis=0).T[:U]
        cols = slice(pair * 128, (pair + 1) * 128)
        slot = 2 * pair + lax.broadcasted_iota(jnp.int32, (U, 128), 1) // R
        out_ref[:, cols] = jnp.where(slot < count[0], far + near_ref[:, cols], 0.0).astype(BF16)


VM = pl.BlockSpec(memory_space=pltpu.VMEM)
SM = pl.BlockSpec(memory_space=pltpu.SMEM)
ANY = pl.BlockSpec(memory_space=pl.ANY)


def per_device(
    sources,
    live_counts,
    aggregate,
    translators,
    boundary_lists,
    far_sources,
    far_translators,
    near_blocks,
    near_columns,
):
    dir_index = lax.axis_index("dir")
    counts = live_counts[0]
    own_count = lax.dynamic_slice(counts, (dir_index,), (1,))
    slot_ids = jnp.arange(S_CL, dtype=jnp.int32)
    live = (slot_ids % BCAP < jnp.repeat(counts, BCAP)).astype(jnp.int32)

    send = pl.pallas_call(
        deal_kernel,
        out_shape=jax.ShapeDtypeStruct((N_DIR, RD * BCAP + KD, 128), BF16),
        in_specs=[VM, VM],
        out_specs=VM,
        scratch_shapes=[pltpu.VMEM((R * BCAP, 128), F32), pltpu.VMEM((KD, 384), F32)],
        name="deal",
    )(sources, translators.T)
    recv = lax.all_to_all(send, "dir", split_axis=0, concat_axis=0, tiled=True)
    recv = pltpu.with_memory_space_constraint(recv, pltpu.VMEM)
    agg = jnp.pad(aggregate.T, ((0, 128 - U), (0, 0)))

    kind_rows, source_rows, groups = pl.pallas_call(
        pack_kernel,
        out_shape=[jax.ShapeDtypeStruct((S_CL, NI), jnp.int32)] * 2
        + [jax.ShapeDtypeStruct((8, S_CL), jnp.int32)],
        in_specs=[SM, VM, VM],
        out_specs=[VM, VM, VM],
        scratch_shapes=[
            pltpu.VMEM((S_CL, NI), jnp.int32),
            pltpu.VMEM((S_CL * 8, NI), F32),
            pltpu.VMEM((S_CL * 8, NI), F32),
        ],
        name="pack",
    )(counts, far_sources, far_translators)
    sent, edge = pl.pallas_call(
        boundary_kernel,
        out_shape=[
            jax.ShapeDtypeStruct((RD * NBND + KC * NHALF, 128), BF16),
            jax.ShapeDtypeStruct((RD * NBND, 128), BF16),
        ],
        in_specs=[VM, VM, VM, ANY],
        out_specs=[VM, VM],
        name="boundary",
    )(recv, boundary_lists.reshape(2 * NBND, 1), live.reshape(1, S_CL), groups)
    clusters = lax.axis_size("clus")
    inner = lax.ppermute(sent, "clus", [(c, c ^ 1) for c in range(clusters)])
    outer = lax.ppermute(edge, "clus", [(c, (c ^ 1) + 2 * (2 * (c % 2) - 1)) for c in range(1, clusters - 1)])
    inner, outer = (pltpu.with_memory_space_constraint(x, pltpu.VMEM) for x in (inner, outer))

    near = pl.pallas_call(
        near_kernel,
        out_shape=jax.ShapeDtypeStruct((U, BCAP * R), F32),
        in_specs=[SM, SM, VM, VM],
        out_specs=VM,
        scratch_shapes=[pltpu.VMEM((BCAP, U, R), BF16), pltpu.VMEM((NN * U, R), BF16)],
        name="near",
    )(near_columns, own_count, sources, near_blocks)
    near = pltpu.with_memory_space_constraint(near, pltpu.VMEM)

    far = pl.pallas_call(
        far_kernel,
        out_shape=jax.ShapeDtypeStruct((N_DIR, (RD - 1) * BCAP, 128), BF16),
        in_specs=[SM, SM, ANY, ANY, VM, VM, VM, VM, VM, VM],
        out_specs=VM,
        scratch_shapes=[
            pltpu.VMEM(((S_EXT + 1) * 16, 128), F32),
            pltpu.VMEM((NTR_PAD * 8, 128), F32),
            pltpu.VMEM((S_CL * 16, 128), F32),
            pltpu.SMEM((S_CL * NI,), jnp.int32),
            pltpu.SMEM((S_CL * NI,), jnp.int32),
            pltpu.SemaphoreType.DMA((N_DIR, 2)),
        ],
        name="far",
    )(
        counts,
        groups,
        kind_rows.reshape(-1),
        source_rows.reshape(-1),
        recv,
        live.reshape(S_CL, 1),
        sent,
        inner,
        outer,
        agg,
    )
    back = lax.all_to_all(far, "dir", split_axis=0, concat_axis=0, tiled=True)
    back = pltpu.with_memory_space_constraint(back, pltpu.VMEM)

    return pl.pallas_call(
        finish_kernel,
        out_shape=jax.ShapeDtypeStruct((U, BCAP * R), BF16),
        in_specs=[SM, VM, VM],
        out_specs=VM,
        scratch_shapes=[pltpu.VMEM((R * BCAP, 128), F32)],
        name="finish",
    )(own_count, back, near)


def solution(mesh):
    in_specs = (
        P(None, ("clus", "dir")),
        P("clus", None),
        P(),
        P(None, "dir"),
        P("clus", None, None),
        P("clus", None),
        P("clus", None),
        P(("clus", "dir"), None, None),
        P(("clus", "dir"), None),
    )
    out_specs = P(None, ("clus", "dir"))
    return jax.shard_map(
        per_device, mesh=mesh, in_specs=in_specs, out_specs=out_specs, check_vma=False
    )
```
